32 devices in a mesh: expert: 8 (over y, x, core), section: 4 (over z).
Axes of the slice: x: 2, y: 2, z: 4, core: 2. Of those that a mesh axis runs over, the one named last changes fastest.
Arguments:
- rows_in: bfloat16 [8, 512, 3072], P('expert', 'section'), may hold values from -6 to 6
- route_prob: float32 [8, 512], P('expert', 'section'), may hold values from 0.2 to 1
- w_in: bfloat16 [8, 128, 8, 3072], P('expert', 'section'), may hold values from -0.109375 to 0.109375
- w_down: bfloat16 [8, 128, 4, 3072], P('expert', 'section'), may hold values from -0.5 to 0.5
- m_send: float32 [8, 48, 3072], P('expert', 'section'), may hold values from -6 to 6
- v_send: float32 [8, 48, 3072], P('expert', 'section'), may hold values from 0.01 to 1
- chosen: int32 [8, 4], P('expert', 'section'), may hold values from 0 to 31
- swap_mask: int32 [4], P('section'), may hold values from 1 to 7, as said below
- dest_slot: int32 [8, 512], P('expert', 'section'), may hold values from 0 to 7, as said below
- dest_row: int32 [8, 512], P('expert', 'section'), may hold values from 0 to 191, as said below
Outputs:
- routed: bfloat16 [8, 768, 3072], P('expert', 'section')
- m_recv: float32 [8, 48, 3072], P('expert', 'section')
- v_recv: float32 [8, 48, 3072], P('expert', 'section')
The draws below stay inside these ranges and needn't reach their ends.
Inputs may be any that keep to these rules, and one draw needn't show every extreme that they name: `swap_mask`: the mask of one section sets every bit of a slot index. `dest_slot`: among the rows of one slot, at most 32 go to one slot of the next section, and one slot of the next section receives 192 rows in all; no slot receives more. `dest_row`: rows arriving at one slot of the next section have distinct destination rows.
All inputs are finite; a program needn't handle non-finite values.
Results may differ from the reference program's by a relative error of at most 0.0049.
Values may be sent and summed in bfloat16 or wider, within the bound.
No kernel may reach another device: no remote copies, remote signals or barrier semaphores. Data moves between devices by JAX's collectives and lax.ppermute only.
A program may use at most 64 MiB of HBM per device.

```python
import math
import jax
import jax.numpy as jnp
from jax import lax

D = 3072
ROWS_DEV = 128
PANELS = 32
PANEL_UNITS = 4
OUT_ROWS = 192
N_EXPERT = 8
N_SECTION = 4


def section_routes(key):
    peer_count = N_EXPERT
    row_count = ROWS_DEV
    out_rows = row_count + row_count // 2
    keys = jax.random.split(key, 5)
    hot_slot = jax.random.randint(keys[0], (), 0, peer_count).astype(jnp.int32)
    shuffled = jax.random.permutation(keys[1], peer_count)
    heavy_src = jnp.zeros((peer_count,), jnp.int32).at[shuffled[:peer_count // 2]].set(1)
    victim = (hot_slot + 1 + jax.random.randint(keys[2], (peer_count,), 0, peer_count - 1)) % peer_count
    sources = jnp.arange(peer_count, dtype=jnp.int32)[:, None]
    positions = jnp.arange(row_count, dtype=jnp.int32)[None, :]
    target = (sources + positions) % peer_count
    redirect = (heavy_src[:, None] == 1) & (target == victim[:, None].astype(jnp.int32))
    target = jnp.where(redirect, hot_slot, target).astype(jnp.int32)
    onehot = (target[:, :, None] == jnp.arange(peer_count, dtype=jnp.int32)[None, None, :]).astype(jnp.int32)
    counts = jnp.sum(onehot, 1)
    before = jnp.cumsum(counts, 0) - counts
    within = jnp.cumsum(onehot, 1) - onehot
    ranks = jnp.sum((before[:, None, :] + within) * onehot, 2).astype(jnp.int32)
    sigma = jax.vmap(lambda sub_key: jax.random.permutation(sub_key, out_rows))(jax.random.split(keys[3], peer_count))
    landing = sigma[target, ranks].astype(jnp.int32)
    order = jax.vmap(lambda sub_key: jax.random.permutation(sub_key, row_count))(jax.random.split(keys[4], peer_count))
    slot_table = jnp.zeros((peer_count, row_count), jnp.int32).at[sources, order].set(target)
    row_table = jnp.zeros((peer_count, row_count), jnp.int32).at[sources, order].set(landing)
    return (slot_table, row_table)


def routing_tables(key):
    keys = jax.random.split(jax.random.fold_in(key, 11), N_SECTION)
    slot_all, row_all = jax.vmap(section_routes)(keys)
    slot_all = jnp.transpose(slot_all, (1, 0, 2)).reshape(N_EXPERT, N_SECTION * ROWS_DEV)
    row_all = jnp.transpose(row_all, (1, 0, 2)).reshape(N_EXPERT, N_SECTION * ROWS_DEV)
    return (slot_all, row_all)


def draw_dest_slot(key, part):
    return routing_tables(key)[0]


def draw_dest_row(key, part):
    return routing_tables(key)[1]


def draw_swap_mask(key, part):
    masks = jax.random.randint(jax.random.fold_in(key, 3), (N_SECTION,), 1, N_EXPERT).astype(jnp.int32)
    which = jax.random.randint(jax.random.fold_in(key, 5), (), 0, N_SECTION)
    return masks.at[which].set(N_EXPERT - 1).astype(jnp.int32)


def set_ends(values, own_key, low, largest):
    place = [jax.random.randint(jax.random.fold_in(own_key, axis), (), 0, length) for axis, length in enumerate(values.shape)]
    main_axis = values.shape.index(max(values.shape))
    neighbour = place[:main_axis] + [(place[main_axis] + 1) % values.shape[main_axis]] + place[main_axis + 1:]
    return values.at[tuple(place)].set(low).at[tuple(neighbour)].set(largest)


def shard_levels(own_key, extent, cuts, least, high):
    level, own = 1.0, jax.random.fold_in(own_key, 6)
    for position, shards_of in cuts:
        draws = jnp.exp(jax.random.uniform(jax.random.fold_in(own, position), (shards_of,), jnp.float32, least / len(cuts), high / len(cuts)))
        level = level * jnp.repeat(draws, extent[position] // shards_of).reshape([-1 if axis == position else 1 for axis in range(len(extent))])
    return level


def gaussian(rng, extent, spread, reach, cuts=(), held_as=jnp.bfloat16):
    drawn = spread * jax.random.normal(rng, extent, jnp.float32)
    if cuts:
        drawn = drawn * shard_levels(rng, extent, cuts, -0.22, 0.18)
    return jnp.clip(drawn, -reach, reach).astype(held_as)


def setup_inputs(seed: int = 0) -> dict:
    seeds = jax.random.split(jax.random.key(seed), 11)
    rows_in = gaussian(seeds[0], (N_EXPERT, N_SECTION * ROWS_DEV, D), 1.0, 6.0, ((0, 8), (1, 4)))
    route_prob = jnp.clip(0.2 + 0.8 * jax.random.uniform(seeds[1], (N_EXPERT, N_SECTION * ROWS_DEV), jnp.float32) ** shard_levels(seeds[1], (N_EXPERT, N_SECTION * ROWS_DEV), ((0, 8), (1, 4)), -0.2, 0.2), 0.2, 1.0)
    w_in = gaussian(seeds[2], (N_EXPERT, N_SECTION * PANELS, 2 * PANEL_UNITS, D), D ** -0.5, 0.109375, ((0, 8), (1, 4)))
    w_down = gaussian(seeds[3], (N_EXPERT, N_SECTION * PANELS, PANEL_UNITS, D), (PANELS * PANEL_UNITS) ** -0.5, 0.5, ((0, 8), (1, 4)))
    m_send = gaussian(seeds[4], (N_EXPERT, N_SECTION * 3 * PANEL_UNITS, D), 1.0, 6.0, ((0, 8), (1, 4)), jnp.float32)
    v_send = jnp.clip(jnp.exp(math.log(1.0) - 4.6051702 * jax.random.uniform(seeds[5], (N_EXPERT, N_SECTION * 3 * PANEL_UNITS, D), jnp.float32) ** shard_levels(seeds[5], (N_EXPERT, N_SECTION * 3 * PANEL_UNITS, D), ((0, 8), (1, 4)), -0.2, 0.2)), 0.01, 1.0)
    chosen = set_ends(jax.random.randint(seeds[6], (N_EXPERT, N_SECTION), 0, PANELS), jax.random.fold_in(seeds[6], 1), 0, PANELS - 1).astype(jnp.int32)
    swap_mask = draw_swap_mask(jax.random.fold_in(seeds[10], 71), 0)
    dest_slot = draw_dest_slot(jax.random.fold_in(seeds[10], 71), 0)
    dest_row = draw_dest_row(jax.random.fold_in(seeds[10], 71), 0)
    return {"rows_in": rows_in, "route_prob": route_prob, "w_in": w_in, "w_down": w_down, "m_send": m_send, "v_send": v_send, "chosen": chosen, "swap_mask": swap_mask, "dest_slot": dest_slot, "dest_row": dest_row}


def expert_block(operands):
    tokens, weight_in, weight_down, scales = operands
    gate_w = weight_in[:, :PANEL_UNITS].reshape(PANELS * PANEL_UNITS, D)
    up_w = weight_in[:, PANEL_UNITS:].reshape(PANELS * PANEL_UNITS, D)
    down_w = weight_down.reshape(PANELS * PANEL_UNITS, D)
    gate_pre = jnp.dot(tokens, gate_w.T, preferred_element_type=jnp.float32)
    up_pre = jnp.dot(tokens, up_w.T, preferred_element_type=jnp.float32)
    hidden = (jax.nn.silu(gate_pre) * up_pre).astype(jnp.bfloat16)
    mixed = jnp.dot(hidden, down_w, preferred_element_type=jnp.float32)
    return (scales[:, None] * mixed).astype(jnp.bfloat16)


def reference(rows_in, route_prob, w_in, w_down, m_send, v_send, chosen, swap_mask, dest_slot, dest_row):
    experts = jnp.arange(N_EXPERT, dtype=jnp.int32)
    panel_in = w_in.reshape(N_EXPERT, N_SECTION, PANELS, 2 * PANEL_UNITS, D)
    panel_down = w_down.reshape(N_EXPERT, N_SECTION, PANELS, PANEL_UNITS, D)
    first = m_send.reshape(N_EXPERT, N_SECTION, 3 * PANEL_UNITS, D)
    second = v_send.reshape(N_EXPERT, N_SECTION, 3 * PANEL_UNITS, D)
    routed = jnp.zeros((N_EXPERT * N_SECTION * OUT_ROWS, D), jnp.bfloat16)
    first_out = []
    second_out = []
    for section in range(N_SECTION):
        partner = jnp.bitwise_xor(experts, swap_mask[section]).astype(jnp.int32)
        own_pick = chosen[:, section].astype(jnp.int32)
        given_panel = own_pick[partner]
        arrive_in = panel_in[partner, section, given_panel]
        arrive_down = panel_down[partner, section, given_panel]
        slot_hit = (jnp.arange(PANELS, dtype=jnp.int32)[None, :] == own_pick[:, None])[:, :, None, None]
        new_in = jnp.where(slot_hit, arrive_in[:, None], panel_in[:, section])
        new_down = jnp.where(slot_hit, arrive_down[:, None], panel_down[:, section])
        first_out.append(first[partner, section])
        second_out.append(second[partner, section])
        tokens = rows_in[:, section * ROWS_DEV:(section + 1) * ROWS_DEV]
        scales = route_prob[:, section * ROWS_DEV:(section + 1) * ROWS_DEV]
        expert_rows = lax.map(expert_block, (tokens, new_in, new_down, scales))
        slot_ids = dest_slot[:, section * ROWS_DEV:(section + 1) * ROWS_DEV].astype(jnp.int32)
        places = dest_row[:, section * ROWS_DEV:(section + 1) * ROWS_DEV].astype(jnp.int32)
        following = (section + 1) % N_SECTION
        flat_index = (slot_ids * N_SECTION + following) * OUT_ROWS + places
        routed = routed.at[flat_index.reshape(-1)].set(expert_rows.reshape(-1, D))
    m_recv = jnp.stack(first_out, 1).reshape(N_EXPERT, N_SECTION * 3 * PANEL_UNITS, D)
    v_recv = jnp.stack(second_out, 1).reshape(N_EXPERT, N_SECTION * 3 * PANEL_UNITS, D)
    return routed.reshape(N_EXPERT, N_SECTION * OUT_ROWS, D), m_recv, v_recv
```

```python
import jax
import jax.numpy as jnp
from jax import lax
from jax.sharding import PartitionSpec as P

LANES = 128


def exchange(arrays, axis, pair_mask):
    size = lax.axis_size(axis)
    low = 0
    while (1 << low) < size:
        bits = min(3, size.bit_length() - 1 - low)
        digit = jnp.bitwise_and(jnp.right_shift(pair_mask, low), (1 << bits) - 1)
        routes = [[(i, i ^ (k << low)) for i in range(size)] for k in range(1 << bits)]
        arms = [lambda held, r=r: [lax.ppermute(x, axis, r) for x in held] for r in routes[1:]]
        arrays = lax.switch(digit, [lambda held: list(held)] + arms, list(arrays))
        low += bits
    return arrays


def rows_times_rows(a, b):
    return lax.dot_general(a, b, (((1,), (1,)), ((), ())), preferred_element_type=jnp.float32)


def columns_times_columns(a, b):
    return lax.dot_general(a, b, (((0,), (0,)), ((), ())), preferred_element_type=jnp.float32)


def per_device(
    rows_in, route_prob, w_in, w_down, m_send, v_send, chosen, swap_mask, dest_slot, dest_row
):
    panels, units2, width = w_in.shape[1:]
    units = units2 // 2
    peers = lax.axis_size("expert")
    sections = lax.axis_size("section")
    tokens = rows_in[0]
    rows = tokens.shape[0]
    capacity = 2 * rows // peers
    out_rows = rows + rows // 2
    panel = chosen[0, 0]
    onward = [(i, (i + 1) % sections) for i in range(sections)]

    pre = rows_times_rows(tokens, w_in[0].reshape(panels * units2, width))
    column = jnp.arange(panels * units2)
    stays = (column % units2 < units) & (column // units2 != panel)
    hidden = jax.nn.silu(pre) * jnp.roll(pre, -units, 1)
    hidden = jnp.where(stays[None], hidden, 0).astype(jnp.bfloat16)
    down = jnp.pad(w_down[0], ((0, 0), (0, units), (0, 0))).reshape(panels * units2, width)
    mixed = jnp.dot(hidden, down, preferred_element_type=jnp.float32)
    base = (route_prob[0][:, None] * mixed).astype(jnp.bfloat16)

    given_in = lax.dynamic_index_in_dim(w_in[0], panel, 0, keepdims=False)
    given_down = lax.dynamic_index_in_dim(w_down[0], panel, 0, keepdims=False)
    given = jnp.concatenate([given_in, given_down], 0)
    base, given, m_held, v_held = lax.optimization_barrier((base, given, m_send[0], v_send[0]))
    arrived_base = lax.ppermute(base, "section", onward)
    taken, m_recv, v_recv = exchange([given, m_held, v_held], "expert", swap_mask[0])

    pre = rows_times_rows(taken[:units2], tokens)
    added = jax.nn.silu(pre[:units]) * pre[units:] * route_prob
    target = dest_slot[0]
    earlier = jnp.arange(rows)[:, None] < jnp.arange(rows)[None, :]
    same = target[:, None] == target[None, :]
    position = jnp.sum((same & earlier).astype(jnp.int32), 0)
    place = (target * capacity + position)[None]
    table = jnp.concatenate(
        [added, (dest_row + 1).astype(jnp.float32), place.astype(jnp.float32)], 0
    ).astype(jnp.bfloat16)
    side = jnp.concatenate([jnp.pad(taken[units2:], ((0, 2), (0, 0))), table], 1)
    side = lax.ppermute(side, "section", onward)

    factors = side[:units, width:]
    label = side[units, width:]
    place = side[units + 1, width:].astype(jnp.int32)
    total = arrived_base + columns_times_columns(factors, side[:units, :width])
    label = jnp.broadcast_to(label[:, None], (rows, LANES))
    payload = jnp.concatenate([total.astype(jnp.bfloat16), label], 1)
    pick = (jnp.arange(peers * capacity)[:, None] == place[None]).astype(jnp.bfloat16)
    packed = jnp.dot(pick, payload, preferred_element_type=jnp.float32).astype(jnp.bfloat16)
    packed = packed.reshape(peers, capacity, width + LANES)
    got = lax.all_to_all(packed, "expert", split_axis=0, concat_axis=0, tiled=True)
    got = got.reshape(peers * capacity, width + LANES)
    labels = got[:, width].astype(jnp.int32)
    put = (jnp.arange(1, out_rows + 1)[:, None] == labels[None]).astype(jnp.bfloat16)
    routed = jnp.dot(put, got[:, :width], preferred_element_type=jnp.float32)
    return (routed.astype(jnp.bfloat16)[None], m_recv[None], v_recv[None])


def solution(mesh):
    spec2, spec3 = P("expert", "section"), P("expert", "section", None)
    spec4 = P("expert", "section", None, None)
    in_specs = (spec3, spec2, spec4, spec4, spec3, spec3, spec2, P("section"), spec2, spec2)
    return jax.shard_map(
        per_device, mesh=mesh, in_specs=in_specs, out_specs=(spec3,) * 3, check_vma=False
    )
```

```python
import jax
import jax.numpy as jnp
from jax import lax
from jax.sharding import PartitionSpec as P

LANES = 128


FIRST, SECOND = 5, 3


def exchange(pair_mask, axis, held, program):
    size = lax.axis_size(axis)
    low = 0
    while True:
        bits = min(3, size.bit_length() - 1 - low)
        last = (1 << (low + bits)) == size
        digit = jnp.bitwise_and(jnp.right_shift(pair_mask, low), (1 << bits) - 1)

        def arm(k, low=low, last=last):
            route = [(i, i ^ (k << low)) for i in range(size)]
            swap = (lambda x: lax.ppermute(x, axis, route)) if k else (lambda x: x)
            return lambda h: program(swap, h) if last else [swap(x) for x in h]

        least = 1 if last and low == 0 else 0
        held = lax.switch(digit - least, [arm(k) for k in range(least, 1 << bits)], held)
        if last:
            return held
        low += bits


def rows_times_rows(a, b):
    return lax.dot_general(a, b, (((1,), (1,)), ((), ())), preferred_element_type=jnp.float32)


def per_device(
    rows_in, route_prob, w_in, w_down, m_send, v_send, chosen, swap_mask, dest_slot, dest_row
):
    panels, units2, width = w_in.shape[1:]
    units = units2 // 2
    peers = lax.axis_size("expert")
    sections = lax.axis_size("section")
    tokens = rows_in[0]
    rows = tokens.shape[0]
    capacity = 2 * rows // peers
    out_rows = rows + rows // 2
    panel = chosen[0, 0]
    onward = [(i, (i + 1) % sections) for i in range(sections)]
    edge = width * FIRST // (FIRST + SECOND)

    def next_section(x):
        return lax.ppermute(x, "section", onward)

    def pick_rows(place, x):
        pick = (jnp.arange(peers * capacity)[:, None] == place[None]).astype(jnp.bfloat16)
        return jnp.dot(pick, x, preferred_element_type=jnp.float32).astype(jnp.bfloat16)

    def put_rows(labels, x):
        put = (jnp.arange(1, out_rows + 1)[:, None] == labels[None]).astype(jnp.bfloat16)
        return jnp.dot(put, x, preferred_element_type=jnp.float32).astype(jnp.bfloat16)

    def deal(packed):
        packed = packed.reshape(peers, capacity, packed.shape[1])
        got = lax.all_to_all(packed, "expert", split_axis=0, concat_axis=0, tiled=True)
        return got.reshape(peers * capacity, got.shape[2])

    def program(swap, held):
        given, m_held, v_held = held
        taken = swap(given)

        pre = rows_times_rows(tokens, w_in[0].reshape(panels * units2, width))
        column = jnp.arange(panels * units2)
        stays = (column % units2 < units) & (column // units2 != panel)
        hidden = jax.nn.silu(pre) * jnp.roll(pre, -units, 1)
        hidden = jnp.where(stays[None], hidden, 0).astype(jnp.bfloat16)
        down = jnp.pad(w_down[0], ((0, 0), (0, units), (0, 0))).reshape(panels * units2, width)
        mixed = jnp.dot(hidden, down, preferred_element_type=jnp.float32)
        taken, mixed = lax.optimization_barrier((taken, mixed))

        pre = rows_times_rows(tokens, taken[:units2])
        hidden = (jax.nn.silu(pre[:, :units]) * pre[:, units:]).astype(jnp.bfloat16)
        mixed = mixed + jnp.dot(hidden, taken[units2:], preferred_element_type=jnp.float32)
        base = (route_prob[0][:, None] * mixed).astype(jnp.bfloat16)

        target = dest_slot[0]
        earlier = jnp.arange(rows)[:, None] < jnp.arange(rows)[None, :]
        same = target[:, None] == target[None, :]
        position = jnp.sum((same & earlier).astype(jnp.int32), 0)
        place = target * capacity + position
        label = jnp.broadcast_to((dest_row[0] + 1).astype(jnp.bfloat16)[:, None], (rows, LANES))

        first, second = base[:, :edge], base[:, edge:]
        m_recv, v_recv = swap(m_held), swap(v_held)
        first, second, places = lax.optimization_barrier((first, second, place))
        first = next_section(first)
        places = next_section(places)
        second, m_recv, v_recv = lax.optimization_barrier((second, m_recv, v_recv))
        second = deal(pick_rows(place, jnp.concatenate([second, label], 1)))
        labels = second[:, width - edge].astype(jnp.int32)
        second = next_section(put_rows(labels, second[:, : width - edge]))
        labels = next_section(labels)
        first = put_rows(labels, deal(pick_rows(places, first)))
        return jnp.concatenate([first, second], 1)[None], m_recv.swapaxes(0, 1), v_recv.swapaxes(0, 1)

    given_in = lax.dynamic_index_in_dim(w_in[0], panel, 0, keepdims=False)
    given_down = lax.dynamic_index_in_dim(w_down[0], panel, 0, keepdims=False)
    given = jnp.concatenate([given_in, given_down], 0)
    return tuple(exchange(swap_mask[0], "expert", [given, m_send.swapaxes(0, 1), v_send.swapaxes(0, 1)], program))


def solution(mesh):
    spec2, spec3 = P("expert", "section"), P("expert", "section", None)
    spec4 = P("expert", "section", None, None)
    in_specs = (spec3, spec2, spec4, spec4, spec3, spec3, spec2, P("section"), spec2, spec2)
    return jax.shard_map(
        per_device, mesh=mesh, in_specs=in_specs, out_specs=(spec3,) * 3, check_vma=False
    )
```

```python
import jax
import jax.numpy as jnp
from jax import lax
from jax.sharding import PartitionSpec as P

LANES = 128


FIRST, SECOND = 2, 1


def exchange(pair_mask, axis, held, program):
    size = lax.axis_size(axis)
    low = 0
    while True:
        bits = min(3, size.bit_length() - 1 - low)
        last = (1 << (low + bits)) == size
        digit = jnp.bitwise_and(jnp.right_shift(pair_mask, low), (1 << bits) - 1)

        def arm(k, low=low, last=last):
            route = [(i, i ^ (k << low)) for i in range(size)]
            swap = (lambda x: lax.ppermute(x, axis, route)) if k else (lambda x: x)
            return lambda h: program(swap, h) if last else [swap(x) for x in h]

        least = 1 if last and low == 0 else 0
        held = lax.switch(digit - least, [arm(k) for k in range(least, 1 << bits)], held)
        if last:
            return held
        low += bits


def rows_times_rows(a, b):
    return lax.dot_general(a, b, (((1,), (1,)), ((), ())), preferred_element_type=jnp.float32)


def per_device(
    rows_in, route_prob, w_in, w_down, m_send, v_send, chosen, swap_mask, dest_slot, dest_row
):
    panels, units2, width = w_in.shape[1:]
    units = units2 // 2
    peers = lax.axis_size("expert")
    sections = lax.axis_size("section")
    tokens = rows_in[0]
    rows = tokens.shape[0]
    capacity = 2 * rows // peers
    out_rows = rows + rows // 2
    panel = chosen[0, 0]
    onward = [(i, (i + 1) % sections) for i in range(sections)]
    edge = width * FIRST // (FIRST + SECOND)

    def next_section(x):
        return lax.ppermute(x, "section", onward)

    def pick_rows(place, x):
        pick = (jnp.arange(peers * capacity)[:, None] == place[None]).astype(jnp.bfloat16)
        return jnp.dot(pick, x, preferred_element_type=jnp.float32).astype(jnp.bfloat16)

    def put_rows(labels, x):
        put = (jnp.arange(1, out_rows + 1)[:, None] == labels[None]).astype(jnp.bfloat16)
        return jnp.dot(put, x, preferred_element_type=jnp.float32).astype(jnp.bfloat16)

    def deal(packed):
        packed = packed.reshape(peers, capacity, packed.shape[1])
        got = lax.all_to_all(packed, "expert", split_axis=0, concat_axis=0, tiled=True)
        return got.reshape(peers * capacity, got.shape[2])

    def program(swap, held):
        given, m_held, v_held = held
        taken = swap(given)

        pre = rows_times_rows(tokens, w_in[0].reshape(panels * units2, width))
        column = jnp.arange(panels * units2)
        stays = (column % units2 < units) & (column // units2 != panel)
        hidden = jax.nn.silu(pre) * jnp.roll(pre, -units, 1)
        hidden = jnp.where(stays[None], hidden, 0).astype(jnp.bfloat16)
        down = jnp.pad(w_down[0], ((0, 0), (0, units), (0, 0))).reshape(panels * units2, width)
        mixed = jnp.dot(hidden, down, preferred_element_type=jnp.float32)
        taken, mixed = lax.optimization_barrier((taken, mixed))

        pre = rows_times_rows(tokens, taken[:units2])
        hidden = (jax.nn.silu(pre[:, :units]) * pre[:, units:]).astype(jnp.bfloat16)
        mixed = mixed + jnp.dot(hidden, taken[units2:], preferred_element_type=jnp.float32)
        base = (route_prob[0][:, None] * mixed).astype(jnp.bfloat16)

        target = dest_slot[0]
        earlier = jnp.arange(rows)[:, None] < jnp.arange(rows)[None, :]
        same = target[:, None] == target[None, :]
        position = jnp.sum((same & earlier).astype(jnp.int32), 0)
        place = target * capacity + position
        label = jnp.broadcast_to((dest_row[0] + 1).astype(jnp.bfloat16)[:, None], (rows, LANES))

        first, second = base[:, :edge], base[:, edge:]
        m_recv, v_recv = swap(m_held), swap(v_held)
        first, second, places = lax.optimization_barrier((first, second, place))
        first = next_section(first)
        places = next_section(places)
        second, m_recv, v_recv = lax.optimization_barrier((second, m_recv, v_recv))
        second = deal(pick_rows(place, jnp.concatenate([second, label], 1)))
        labels = second[:, width - edge].astype(jnp.int32)
        second = next_section(put_rows(labels, second[:, : width - edge]))
        labels = next_section(labels)
        first = put_rows(labels, deal(pick_rows(places, first)))
        return jnp.concatenate([first, second], 1)[None], m_recv.swapaxes(0, 1), v_recv.swapaxes(0, 1)

    given_in = lax.dynamic_index_in_dim(w_in[0], panel, 0, keepdims=False)
    given_down = lax.dynamic_index_in_dim(w_down[0], panel, 0, keepdims=False)
    given = jnp.concatenate([given_in, given_down], 0)
    return tuple(exchange(swap_mask[0], "expert", [given, m_send.swapaxes(0, 1), v_send.swapaxes(0, 1)], program))


def solution(mesh):
    spec2, spec3 = P("expert", "section"), P("expert", "section", None)
    spec4 = P("expert", "section", None, None)
    in_specs = (spec3, spec2, spec4, spec4, spec3, spec3, spec2, P("section"), spec2, spec2)
    return jax.shard_map(
        per_device, mesh=mesh, in_specs=in_specs, out_specs=(spec3,) * 3, check_vma=False
    )
```
